256 devices in a mesh: row: 32 (over z, y), col: 8 (over x, core).
Axes of the slice: x: 4, y: 4, z: 8, core: 2. Of those that a mesh axis runs over, the one named last changes fastest.
Arguments:
- covariance: float32 [16384, 16384], P('row', 'col'), as said below
- courant: float32 [2, 16384], replicated, may hold values from 0.05 to 0.45
- upwind: int32 [16384], replicated, may hold values from 0 to 3
- observed: int32 [2, 256], replicated, may hold values from 0 to 16383
- noise: float32 [2, 256], replicated, may hold values from 0.5 to 2
Outputs:
- posterior: float32 [16384, 16384], P('row', 'col')
The draws below stay inside these ranges and needn't reach their ends.
Inputs may be any that keep to these rules, and one draw needn't show every extreme that they name: The covariance is symmetric and positive definite.
All inputs are finite; a program needn't handle non-finite values.
Results may differ from the reference program's by a relative error of at most 0.0003.
Values sent between devices are 32-bit elements; how exact they have to be, the bound alone decides.
No kernel may reach another device: no remote copies, remote signals or barrier semaphores. Data moves between devices by JAX's collectives and lax.ppermute only.
A program may use at most 64 MiB of HBM per device.

```python
import math
import jax
import jax.numpy as jnp
from jax import lax

G = 128
KOBS = 256
BATCHES = 2
NC = 16384


def smooth_fields(white, lengths):
    base = jnp.arange(G, dtype=jnp.float32)
    spacing = base[:, None] - base[None, :]
    kernels = jnp.exp(-spacing[None, :, :] ** 2 / (2.0 * lengths[:, None, None] ** 2))
    first = jnp.einsum('jab,jbc->jac', kernels, white, precision=lax.Precision.HIGHEST)
    fields = jnp.einsum('jac,jdc->jad', first, kernels, precision=lax.Precision.HIGHEST)
    spread = jnp.sqrt(jnp.mean(fields * fields, axis=(1, 2), keepdims=True) + 1e-12)
    return fields / spread


def draw_covariance(key, part):
    total = G * G
    count = min(2048, total)
    keys = jax.random.split(jax.random.fold_in(key, 7), 4)
    white = jax.random.normal(keys[0], (count, G, G), jnp.float32)
    lengths = jnp.exp(jax.random.uniform(keys[1], (count,), jnp.float32, math.log(max(1.0, G / 32.0)), math.log(G / 4.0)))
    amplitude = jnp.exp(jax.random.uniform(keys[2], (total,), jnp.float32, math.log(0.5), math.log(2.0)))
    floor_vals = jnp.exp(jax.random.uniform(keys[3], (total,), jnp.float32, math.log(0.25), math.log(1.0)))
    fields = smooth_fields(white, lengths)
    basis = fields.reshape(count, total) * amplitude[None, :]
    gram = jnp.dot(basis.T, basis, precision=lax.Precision.HIGHEST, preferred_element_type=jnp.float32) / count
    gram = 0.5 * (gram + gram.T)
    cells = jnp.arange(total)
    return gram.at[cells, cells].add(floor_vals)


def touch_ends(result, stream_key, smallest, largest):
    spot = [jax.random.randint(jax.random.fold_in(stream_key, axis), (), 0, length) for axis, length in enumerate(result.shape)]
    main_axis = result.shape.index(max(result.shape))
    neighbour = spot[:main_axis] + [(spot[main_axis] + 1) % result.shape[main_axis]] + spot[main_axis + 1:]
    return result.at[tuple(spot)].set(smallest).at[tuple(neighbour)].set(largest)


def setup_inputs(seed: int = 0) -> dict:
    seeds = jax.random.split(jax.random.key(seed), 6)
    return {
        "covariance": draw_covariance(jax.random.fold_in(seeds[5], 71), 0),
        "courant": jnp.clip(jax.random.uniform(seeds[1], (2, NC), jnp.float32, 0.05, 0.45), 0.05, 0.45),
        "upwind": touch_ends(jax.random.randint(seeds[2], (NC,), 0, 4), jax.random.fold_in(seeds[2], 1), 0, 3).astype(jnp.int32),
        "observed": touch_ends(jax.random.randint(seeds[3], (BATCHES, KOBS), 0, NC), jax.random.fold_in(seeds[3], 1), 0, NC - 1).astype(jnp.int32),
        "noise": jnp.clip(jnp.exp(jax.random.uniform(seeds[4], (BATCHES, KOBS), jnp.float32, math.log(0.5), math.log(2.0))), 0.5, 2.0),
    }


def left_apply(padded, cour_a, cour_b, up_dir):
    lines = padded.shape[0] - 2
    center = padded[1:-1]
    prev_line = padded[:-2]
    next_line = padded[2:]
    prev_cell = jnp.pad(center, ((0, 0), (1, 0), (0, 0)))[:, :-1]
    next_cell = jnp.pad(center, ((0, 0), (0, 1), (0, 0)))[:, 1:]
    coef_a = cour_a.reshape(lines, G, 1)
    coef_b = cour_b.reshape(lines, G, 1)
    dirs = up_dir.reshape(lines, G, 1)
    up_line = jnp.where(dirs % 2 == 1, next_line, prev_line)
    up_cell = jnp.where(dirs // 2 == 1, next_cell, prev_cell)
    return (1.0 - coef_a - coef_b) * center + coef_a * up_line + coef_b * up_cell

def right_apply(padded, cour_a, cour_b, up_dir):
    lines = padded.shape[1] - 2
    center = padded[:, 1:-1]
    prev_line = padded[:, :-2]
    next_line = padded[:, 2:]
    prev_cell = jnp.pad(center, ((0, 0), (0, 0), (1, 0)))[:, :, :-1]
    next_cell = jnp.pad(center, ((0, 0), (0, 0), (0, 1)))[:, :, 1:]
    coef_a = cour_a.reshape(1, lines, G)
    coef_b = cour_b.reshape(1, lines, G)
    dirs = up_dir.reshape(1, lines, G)
    up_line = jnp.where(dirs % 2 == 1, next_line, prev_line)
    up_cell = jnp.where(dirs // 2 == 1, next_cell, prev_cell)
    return (1.0 - coef_a - coef_b) * center + coef_a * up_line + coef_b * up_cell

def reference(covariance, courant, upwind, observed, noise):
    total = G * G
    state = covariance
    for cycle in range(BATCHES):
        padded = jnp.pad(state.reshape(G, G, total), ((1, 1), (0, 0), (0, 0)))
        state = left_apply(padded, courant[0], courant[1], upwind).reshape(total, total)
        padded = jnp.pad(state.reshape(total, G, G), ((0, 0), (1, 1), (0, 0)))
        state = right_apply(padded, courant[0], courant[1], upwind).reshape(total, total)
        obs = observed[cycle]
        col_panel = jnp.take(state, obs, axis=1)
        row_panel = jnp.take(state, obs, axis=0)
        innov = jnp.take(row_panel, obs, axis=1) + jnp.diag(noise[cycle])
        factor = jnp.linalg.cholesky(innov)
        gain = jax.scipy.linalg.cho_solve((factor, True), col_panel.T).T
        state = state - jnp.dot(gain.astype(jnp.float32), row_panel.astype(jnp.float32), precision=lax.Precision.HIGHEST, preferred_element_type=jnp.float32)
    return state
```

```python
import jax
import jax.numpy as jnp
from jax import lax
from jax.experimental import pallas as pl
from jax.experimental.pallas import tpu as pltpu
from jax.sharding import Mesh, PartitionSpec as P

G = 128
BATCHES = 2
KOBS = 256
HALO = BATCHES * G
ALL = ("z", "y", "x", "k")
COL = ("x", "k")
NB = 128
F32 = jnp.float32


def mm(a, b, dims):
    return lax.dot_general(
        a, b, (dims, ((), ())), precision=lax.Precision.HIGHEST, preferred_element_type=F32
    )


def call(kernel, out_shape, flops, moved, **kw):
    return pl.pallas_call(
        kernel,
        out_shape=out_shape,
        cost_estimate=pl.CostEstimate(flops=flops, bytes_accessed=moved, transcendentals=0),
        **kw,
    )


def lookup(table, line, pos):
    n = line.shape[0]
    lane = lax.broadcasted_iota(jnp.int32, (n, G), 1)
    picked = mm((lane == line).astype(F32), table, ((1,), (0,)))
    hit = lane == pos
    parts = [
        jnp.sum(jnp.where(hit, picked[:, i * G : (i + 1) * G], 0.0), axis=1, keepdims=True)
        for i in range(3)
    ]
    return parts


def spread_taps(table, line, pos):
    a, b, u = lookup(table, line, pos)
    code = u.astype(jnp.int32)
    line2 = line + jnp.where(code % 2 == 1, 1, -1)
    pos2 = pos + jnp.where(code // 2 == 1, 1, -1)
    wl = jnp.where((line2 >= 0) & (line2 < G), a, 0.0)
    wc = jnp.where((pos2 >= 0) & (pos2 < G), b, 0.0)
    return [(line, pos, 1.0 - a - b), (line2, pos, wl), (line, pos2, wc)]


def tap_tile(idx_ref, w_ref, base, width):
    cell = lax.broadcasted_iota(jnp.int32, (KOBS, width), 1) + base
    halves = []
    for half, count in ((0, 3), (1, 9)):
        rows = slice(half * KOBS, (half + 1) * KOBS)
        acc = None
        for m in range(count):
            term = jnp.where(cell == idx_ref[rows, m : m + 1], w_ref[rows, m : m + 1], 0.0)
            acc = term if acc is None else acc + term
        halves.append(acc)
    return jnp.concatenate(halves, axis=0)


def project_kernel(start_ref, obs_ref, table_ref, p_ref, h_ref, idx_ref, w_ref):
    step = pl.program_id(0)
    width = p_ref.shape[1]

    @pl.when(step == 0)
    def _():
        table = table_ref[...]
        obs = obs_ref[...]
        first = spread_taps(table, obs // G, obs % G)
        lane = lax.broadcasted_iota(jnp.int32, (KOBS, 128), 1)
        for half in range(2):
            rows = slice(half * KOBS, (half + 1) * KOBS)
            taps = [(l[rows], p[rows], w[rows]) for l, p, w in first]
            if half == 1:
                taps = [
                    (l2, p2, w * w2)
                    for l, p, w in taps
                    for l2, p2, w2 in spread_taps(table, l, p)
                ]
            idx = jnp.zeros((KOBS, 128), jnp.int32)
            wts = jnp.zeros((KOBS, 128), F32)
            for m, (l, p, w) in enumerate(taps):
                idx = jnp.where(lane == m, l * G + p, idx)
                wts = jnp.where(lane == m, w, wts)
            idx_ref[rows, :] = idx
            w_ref[rows, :] = wts
        h_ref[...] = jnp.zeros_like(h_ref)

    tile = tap_tile(idx_ref, w_ref, start_ref[1] + step * width, width)
    h_ref[...] += mm(tile, p_ref[...], ((1,), (1,)))


def project(starts, obs, table, block):
    rows, cols = block.shape
    n = obs.shape[0]
    width = 256
    return call(
        project_kernel,
        (
            jax.ShapeDtypeStruct((n, rows), F32),
            jax.ShapeDtypeStruct((n, 128), jnp.int32),
            jax.ShapeDtypeStruct((n, 128), F32),
        ),
        2 * n * rows * cols * 6,
        4 * rows * cols,
        grid_spec=pltpu.PrefetchScalarGridSpec(
            num_scalar_prefetch=1,
            grid=(cols // width,),
            in_specs=[
                pl.BlockSpec((n, 1), lambda i, s: (0, 0)),
                pl.BlockSpec(table.shape, lambda i, s: (0, 0)),
                pl.BlockSpec((rows, width), lambda i, s: (0, i)),
            ],
            out_specs=[
                pl.BlockSpec((n, rows), lambda i, s: (0, 0)),
                pl.BlockSpec((n, 128), lambda i, s: (0, 0)),
                pl.BlockSpec((n, 128), lambda i, s: (0, 0)),
            ],
        ),
        name="project",
    )(starts, obs, table, block)


def innov_kernel(start_ref, parts_ref, idx_ref, w_ref, h_ref, t_ref):
    h = parts_ref[0]
    for i in range(1, parts_ref.shape[0]):
        h = h + parts_ref[i]
    h_ref[...] = h
    tile = tap_tile(idx_ref, w_ref, start_ref[0], h.shape[1])
    t_ref[...] = mm(h, tile, ((1,), (1,)))


def innov(starts, parts, idx, w):
    count, some, rows = parts.shape
    n = idx.shape[0]
    vmem = pl.BlockSpec(memory_space=pltpu.VMEM)
    return call(
        innov_kernel,
        (jax.ShapeDtypeStruct((some, rows), F32), jax.ShapeDtypeStruct((some, n), F32)),
        2 * some * rows * n * 6,
        4 * count * some * rows,
        in_specs=[pl.BlockSpec(memory_space=pltpu.SMEM), vmem, vmem, vmem],
        out_specs=[vmem, vmem],
        name="innov",
    )(starts, parts, idx, w)


def stencil(v, coef, axis):
    n = v.shape[axis]
    c, nl, pv, nc, pc = coef
    return (
        c * v
        + nl * pltpu.roll(v, n - G, axis)
        + pv * pltpu.roll(v, G, axis)
        + nc * pltpu.roll(v, n - 1, axis)
        + pc * pltpu.roll(v, 1, axis)
    )


def along_lanes(coef_ref):
    return [coef_ref[i : i + 1, :] for i in range(5)]


def panel_kernel(lo_ref, h_ref, hi_ref, coef_ref, g_ref):
    v = jnp.concatenate([lo_ref[...], h_ref[...], hi_ref[...]], axis=1)
    coef = along_lanes(coef_ref)
    for _ in range(BATCHES):
        v = stencil(v, coef, 1)
    g_ref[...] = v[:, HALO:-HALO]


def panel(lo, h, hi, coef):
    return call(
        panel_kernel, jax.ShapeDtypeStruct(h.shape, F32), 20 * h.size, 16 * h.size, name="panel"
    )(lo, h, hi, coef)


def left_kernel(lo_ref, p_ref, hi_ref, coef_ref, out_ref):
    v = jnp.concatenate([lo_ref[...], p_ref[...], hi_ref[...]], axis=0)
    coef = [coef_ref[:, i : i + 1] for i in range(5)]
    for _ in range(BATCHES):
        v = stencil(v, coef, 0)
    out_ref[...] = v[HALO:-HALO, :]


def left(lo, block, hi, coef):
    rows, cols = block.shape
    width = 256
    spec = lambda r: pl.BlockSpec((r, width), lambda i: (0, i))
    return call(
        left_kernel,
        jax.ShapeDtypeStruct(block.shape, F32),
        40 * block.size,
        12 * block.size,
        grid=(cols // width,),
        in_specs=[spec(HALO), spec(rows), spec(HALO), pl.BlockSpec(coef.shape, lambda i: (0, 0))],
        out_specs=spec(rows),
        name="left",
    )(lo, block, hi, coef)


def final_kernel(lo_ref, l_ref, hi_ref, coef_ref, z_ref, g_ref, out_ref):
    v = jnp.concatenate([lo_ref[...], l_ref[...], hi_ref[...]], axis=1)
    coef = along_lanes(coef_ref)
    for _ in range(BATCHES):
        v = stencil(v, coef, 1)
    out_ref[...] = v[:, HALO:-HALO] - mm(z_ref[...], g_ref[...], ((0,), (0,)))


def final(lo, block, hi, coef, z, g):
    rows, cols = block.shape
    n = z.shape[0]
    height = 128
    spec = lambda c: pl.BlockSpec((height, c), lambda i: (i, 0))
    return call(
        final_kernel,
        jax.ShapeDtypeStruct(block.shape, F32),
        2 * n * rows * cols * 6,
        16 * block.size,
        grid=(rows // height,),
        in_specs=[
            spec(HALO),
            spec(cols),
            spec(HALO),
            pl.BlockSpec(coef.shape, lambda i: (0, 0)),
            pl.BlockSpec((n, height), lambda i: (0, i)),
            pl.BlockSpec(g.shape, lambda i: (0, 0)),
        ],
        out_specs=spec(cols),
        name="final",
    )(lo, block, hi, coef, z, g)


def diag_inverse(block):
    n = block.shape[0]
    tiles = n // 8
    lane = lax.broadcasted_iota(jnp.int32, (8, n), 1)
    sub = lax.broadcasted_iota(jnp.int32, (8, n), 0)
    d = [block[8 * t : 8 * t + 8] for t in range(tiles)]
    b = [(lane == sub + 8 * t).astype(F32) for t in range(tiles)]
    spread = lambda v: jnp.broadcast_to(v, (8, n))
    for p in range(tiles):
        row = [spread(d[p][s : s + 1]) for s in range(8)]
        brow = [spread(b[p][s : s + 1]) for s in range(8)]
        m = [[spread(row[r][:, 8 * p + s : 8 * p + s + 1]) for s in range(r + 1)] for r in range(8)]
        inv, low = [], []
        for s in range(8):
            inv.append(lax.rsqrt(m[s][s]))
            low.append([None] * (s + 1) + [m[r][s] * inv[s] for r in range(s + 1, 8)])
            for r in range(s + 1, 8):
                for q in range(s + 1, r + 1):
                    m[r][q] = m[r][q] - low[s][r] * low[s][q]
            row[s] = row[s] * inv[s]
            brow[s] = brow[s] * inv[s]
            for r in range(s + 1, 8):
                row[r] = row[r] - low[s][r] * row[s]
                brow[r] = brow[r] - low[s][r] * brow[s]
        out = brow[0]
        for s in range(1, 8):
            out = jnp.where(sub == s, brow[s], out)
        b[p] = out
        for s in reversed(range(8)):
            for r in range(s + 1, 8):
                row[s] = row[s] - low[s][r] * row[r]
                brow[s] = brow[s] - low[s][r] * brow[r]
            row[s] = row[s] * inv[s]
            brow[s] = brow[s] * inv[s]
        for t in range(p + 1, tiles):
            raw = d[t]
            for s in range(8):
                col = spread(raw[:, 8 * p + s : 8 * p + s + 1])
                d[t] = d[t] - col * row[s]
                b[t] = b[t] - col * brow[s]
    return jnp.concatenate(b, axis=0)


def factor_kernel(cov_ref, noise_ref, inv_ref, up_ref):
    n = cov_ref.shape[0]
    eye = lax.broadcasted_iota(jnp.int32, (n, n), 0) == lax.broadcasted_iota(jnp.int32, (n, n), 1)
    up_ref[...] = cov_ref[...] + jnp.where(eye, noise_ref[...], 0.0)
    for k in range(n // NB):
        lo, hi = k * NB, (k + 1) * NB
        linv = diag_inverse(up_ref[lo:hi, lo:hi])
        inv_ref[k] = linv
        if hi < n:
            w = mm(linv, up_ref[lo:hi, hi:], ((1,), (0,)))
            up_ref[lo:hi, hi:] = w
            up_ref[hi:, hi:] = up_ref[hi:, hi:] - mm(w, w, ((0,), (0,)))


def factor(cov, noise):
    n = cov.shape[0]
    return call(
        factor_kernel,
        (jax.ShapeDtypeStruct((n // NB, NB, NB), F32), jax.ShapeDtypeStruct((n, n), F32)),
        15 * 10**9,
        8 * cov.size,
        name="factor",
    )(cov, noise)


def solve_kernel(inv_ref, up_ref, g_ref, z_ref):
    blocks = up_ref.shape[0] // NB
    at = lambda i: slice(i * NB, (i + 1) * NB)
    ys = []
    for k in range(blocks):
        acc = g_ref[at(k), :]
        for i in range(k):
            acc = acc - mm(up_ref[at(i), at(k)], ys[i], ((0,), (0,)))
        ys.append(mm(inv_ref[k], acc, ((1,), (0,))))
    zs = [None] * blocks
    for k in reversed(range(blocks)):
        acc = ys[k]
        for i in range(k + 1, blocks):
            acc = acc - mm(up_ref[at(k), at(i)], zs[i], ((1,), (0,)))
        zs[k] = mm(inv_ref[k], acc, ((0,), (0,)))
        z_ref[at(k), :] = zs[k]


def solve(inv, up, g):
    return call(
        solve_kernel, jax.ShapeDtypeStruct(g.shape, F32), 4 * 10**9, 16 * g.size, name="solve"
    )(inv, up, g)


def neighbours(v_low, v_high, axis):
    count = lax.axis_size(axis)
    forward = [(i, i + 1) for i in range(count - 1)]
    backward = [(t, s) for s, t in forward]
    return lax.ppermute(v_high, axis, forward), lax.ppermute(v_low, axis, backward)


def shards(covariance, courant, upwind, observed, noise):
    rows, cols = covariance.shape
    row_start = lax.axis_index(("z", "y")) * rows
    col_start = lax.axis_index(COL) * cols
    starts = jnp.stack([row_start, col_start]).astype(jnp.int32)
    depth, planes = lax.axis_size("z"), lax.axis_size("y")
    across = lax.axis_size(COL)

    top, bottom = neighbours(covariance[:HALO], covariance[-HALO:], ("z", "y"))

    table = jnp.concatenate(
        [courant.reshape(2, G, G), upwind.reshape(1, G, G).astype(F32)], axis=0
    )
    table = table.transpose(1, 0, 2).reshape(G, 3 * G)
    obs = observed.reshape(-1, 1)
    partial, idx, w = project(starts, obs, table, covariance)
    some = partial.shape[0] // across
    parts = lax.all_to_all(partial.reshape(across, some, rows), COL, 0, 0, tiled=True)
    h, t = innov(starts, parts, idx, w)

    t = lax.all_to_all(t.reshape(depth, some // depth, -1), "z", 0, 0, tiled=True).sum(0)
    t = lax.all_gather(t, "y", axis=0).sum(0)
    t = lax.all_gather(t, "z", axis=0, tiled=True)
    t = lax.all_to_all(jnp.broadcast_to(t[None], (across,) + t.shape), COL, 0, 0, tiled=True)
    cov = t.reshape(BATCHES * KOBS, BATCHES * KOBS)

    a, b = courant[0], courant[1]
    line_up, cell_up = upwind % 2 == 1, upwind // 2 == 1
    pos = jnp.arange(a.shape[0]) % G
    coef = jnp.stack(
        [
            1.0 - a - b,
            jnp.where(line_up, a, 0.0),
            jnp.where(line_up, 0.0, a),
            jnp.where(cell_up & (pos < G - 1), b, 0.0),
            jnp.where(cell_up | (pos == 0), 0.0, b),
        ]
    )
    coef = jnp.pad(coef, ((0, 3), (HALO, HALO)))
    row_coef = lax.dynamic_slice_in_dim(coef, row_start, rows + 2 * HALO, 1)
    col_coef = lax.dynamic_slice_in_dim(coef, col_start, cols + 2 * HALO, 1)

    before, after = neighbours(h[:, :HALO], h[:, -HALO:], ("z", "y"))
    g = panel(before, h, after, row_coef)
    g_rows = lax.all_gather(g, COL, axis=0, tiled=True)
    turn = [
        ((z * planes + y) * across + c, (c * planes + y) * across + z)
        for z in range(depth)
        for y in range(planes)
        for c in range(across)
    ]
    g_cols = lax.ppermute(g, ALL, turn)
    g_cols = lax.all_gather(g_cols, "y", axis=1, tiled=True)
    g_cols = lax.all_gather(g_cols, "z", axis=0, tiled=True)

    top, bottom, cov = lax.optimization_barrier((top, bottom, cov))
    moved = left(top, covariance, bottom, row_coef.T)
    before, after = neighbours(moved[:, :HALO], moved[:, -HALO:], COL)
    inv, up = factor(cov, noise.reshape(1, -1))
    z = solve(inv, up, g_rows)
    return final(before, moved, after, col_coef, z, g_cols)


def solution(mesh):
    fine = Mesh(mesh.devices.reshape(8, 4, 4, 2), ALL)
    spec = P(("z", "y"), COL)
    return jax.shard_map(
        shards, mesh=fine, in_specs=(spec, P(), P(), P(), P()), out_specs=spec, check_vma=False
    )
```
